32 devices in a mesh: section: 4 (over y, core), expert: 8 (over z, x).
Axes of the slice: x: 2, y: 2, z: 4, core: 2. Of those that a mesh axis runs over, the one named last changes fastest.
Arguments:
- tokens: bfloat16 [1024, 3584], P('expert', 'section'), may hold values from -6 to 6
- expert_ids: int32 [1024, 2], P('expert'), may hold values from 0 to 7, all different within a row; in each aligned block of 128 rows (0 to 127, 128 to 255, ...) at most 48 rows name the same one
- gates: float32 [1024, 2], P('expert'), may hold values from 0.02 to 0.4
- cotangent: bfloat16 [1024, 3584], P('expert', 'section'), may hold values from -6 to 6
- w_gate: bfloat16 [8, 3584, 1024], P('expert', 'section'), may hold values from -0.09375 to 0.09375
- w_up: bfloat16 [8, 3584, 1024], P('expert', 'section'), may hold values from -0.09375 to 0.09375
- w_down: bfloat16 [8, 1024, 3584], P('expert', None, 'section'), may hold values from -0.1875 to 0.1875
Outputs:
- mixed: bfloat16 [1024, 3584], P('expert', 'section')
- token_grads: bfloat16 [1024, 3584], P('expert', 'section')
- down_grads: bfloat16 [8, 1024, 3584], P('expert', None, 'section')
The draws below stay inside these ranges and needn't reach their ends.
Inputs may be any that keep to these rules, and one draw needn't show every extreme that they name: `expert_ids`: within each aligned block of 128 rows no expert is named more than 48 times, a bound that some block reaches; the 2 experts of a row differ.
All inputs are finite; a program needn't handle non-finite values.
Results may differ from the reference program's by a relative error of at most 0.024.
Values may be sent and summed in bfloat16 or wider, within the bound.
A program may use at most 64 MiB of HBM per device.

```python
import math
import jax
import jax.numpy as jnp
import numpy as np
from jax import lax

D = 3584
HID = 1024
TOPK = 2
TOK_DEV = 128
EXPERTS = 8
CAP = 48
DC = 896
TOKENS = 1024
N_SECTION = 4
N_EXPERT = 8


def block_scale(own_key, shape, cuts, smallest, top_value):
    gain, own = 1.0, jax.random.fold_in(own_key, 6)
    for position, blocks in cuts:
        draws = jnp.exp(jax.random.uniform(jax.random.fold_in(own, position), (blocks,), jnp.float32, smallest / len(cuts), top_value / len(cuts)))
        gain = gain * jnp.repeat(draws, shape[position] // blocks).reshape([-1 if axis == position else 1 for axis in range(len(shape))])
    return gain


def shared_out(stream_key, own, number, rows, number_of, top, limit, skew):
    sequence = jax.random.permutation(stream_key, number_of)
    crowded, usual = load_shares(number_of, rows * top, limit, skew, True), load_shares(number_of, rows * top, limit, skew, False)
    places = jnp.arange(number_of)

    def named(sizes, offset_by):
        used = int((sizes > 0).sum())
        fixed = max(1, used // 4)
        shifted = fixed + (places - fixed + offset_by * (used - fixed)) % max(1, number_of - fixed)
        return jnp.zeros((number_of,), jnp.int32).at[sequence[jnp.where(places < fixed, places, shifted)]].set(jnp.asarray(sizes, jnp.int32))

    sizes = jnp.where(number % 4 == 0, named(crowded, number // 4), named(usual, number - number // 4 - 1))
    mixed = jax.random.permutation(jax.random.fold_in(own, 3), number_of)
    giver, sink = mixed[0:number_of // 2 * 2:2], mixed[1:number_of // 2 * 2:2]
    margin = jnp.minimum(sizes[giver] - 1, limit - sizes[sink]) // 2
    margin = jnp.where((giver == sequence[0]) | (sink == sequence[0]) | (sizes[sink] == 0), 0, jnp.maximum(margin, 0))
    shifted = jax.random.randint(jax.random.fold_in(own, 4), (number_of // 2,), 0, 1 << 20) % (margin + 1)
    sizes = sizes.at[giver].add(-shifted).at[sink].add(shifted)
    items = jnp.searchsorted(jnp.cumsum(sizes), jnp.arange(rows * top), side="right").astype(jnp.int32)
    listing = items.reshape(top, rows).T
    listing = listing[jax.random.permutation(jax.random.fold_in(own, 1), rows)]
    offset_by = jax.random.randint(jax.random.fold_in(own, 2), (rows, 1), 0, top)
    return jnp.take_along_axis(listing, (jnp.arange(top)[None, :] + offset_by) % top, axis=1)


def load_shares(number_of, total, reach, slope, full):
    portions = [(1 << 20) // math.isqrt(rank ** slope) + 1 for rank in range(1, number_of + 1)]
    largest = reach if full else min(reach, max(-(-total // number_of), total * portions[0] // sum(portions)))
    least = 1 if total - largest >= number_of - 1 else 0
    holding, spare = [largest] + [least] * (number_of - 1), total - largest - least * (number_of - 1)
    while spare > 0:
        candidates = [i for i in range(1, number_of) if holding[i] < largest] or [i for i in range(1, number_of) if holding[i] < reach]
        mass, remaining = sum([portions[i] for i in candidates]), spare
        for i in candidates:
            more = min(reach - holding[i], max(1, remaining * portions[i] // mass), spare)
            holding[i] = holding[i] + more
            spare = spare - more
    return np.array(holding)


def bell_draw(own_key, dims, width, bound, shards=(), kind=jnp.bfloat16):
    array = width * jax.random.normal(own_key, dims, jnp.float32)
    if shards:
        array = array * block_scale(own_key, dims, shards, -0.22, 0.18)
    return jnp.clip(array, -bound, bound).astype(kind)


def setup_inputs(seed: int = 0) -> dict:
    streams_of = jax.random.split(jax.random.key(seed), 8)
    tokens = bell_draw(streams_of[0], (TOKENS, D), 1.0, 6.0, ((0, 8), (1, 4)))
    expert_ids_keys = jax.random.split(jax.random.fold_in(streams_of[1], 1), TOKENS // TOK_DEV)
    expert_ids_turns = jax.random.permutation(jax.random.fold_in(streams_of[1], 3), TOKENS // TOK_DEV)
    expert_ids = jax.vmap(lambda own, number: shared_out(jax.random.fold_in(streams_of[1], 2), own, number, TOK_DEV, EXPERTS, TOPK, CAP, 2))(expert_ids_keys, expert_ids_turns).reshape((TOKENS, TOPK))
    gates = jnp.clip(jnp.exp(math.log(0.4) - 2.9957323 * jax.random.uniform(streams_of[2], (TOKENS, TOPK), jnp.float32) ** block_scale(streams_of[2], (TOKENS, TOPK), ((0, 8),), -0.2, 0.2)), 0.02, 0.4)
    cotangent = bell_draw(streams_of[3], (TOKENS, D), 1.0, 6.0, ((0, 8), (1, 4)))
    w_gate = bell_draw(streams_of[4], (EXPERTS, D, HID), D ** -0.5, 0.09375, ((0, 8), (1, 4)))
    w_up = bell_draw(streams_of[5], (EXPERTS, D, HID), D ** -0.5, 0.09375, ((0, 8), (1, 4)))
    w_down = bell_draw(streams_of[6], (EXPERTS, HID, D), HID ** -0.5, 0.1875, ((0, 8), (2, 4)))
    return {"tokens": tokens, "expert_ids": expert_ids, "gates": gates, "cotangent": cotangent, "w_gate": w_gate, "w_up": w_up, "w_down": w_down}


def rounded_groups(left, right, form):
    parts = jnp.einsum(form, left, right).astype(jnp.bfloat16)
    return jnp.sum(parts.astype(jnp.float32), axis=0)


def expert_pass(packed):
    rows, grads, gate_w, up_w, down_w = packed
    row_split = rows.astype(jnp.float32).reshape(-1, N_SECTION, DC)
    grad_split = grads.astype(jnp.float32).reshape(-1, N_SECTION, DC)
    gate_pre = rounded_groups(row_split, gate_w.astype(jnp.float32).reshape(N_SECTION, DC, HID), "rsc,sch->srh")
    up_pre = rounded_groups(row_split, up_w.astype(jnp.float32).reshape(N_SECTION, DC, HID), "rsc,sch->srh")
    sigmoid_val = jax.nn.sigmoid(gate_pre)
    activated = gate_pre * sigmoid_val
    hidden = (activated * up_pre).astype(jnp.bfloat16)
    outputs = jnp.dot(hidden, down_w, preferred_element_type=jnp.float32).astype(jnp.bfloat16)
    hidden_grad = rounded_groups(grad_split, down_w.astype(jnp.float32).reshape(HID, N_SECTION, DC), "rsc,hsc->srh")
    down_grad = jnp.dot(hidden.T, grads, preferred_element_type=jnp.float32).astype(jnp.bfloat16)
    gate_grad = (hidden_grad * up_pre * sigmoid_val * (1.0 + gate_pre * (1.0 - sigmoid_val))).astype(jnp.bfloat16)
    up_grad = (hidden_grad * activated).astype(jnp.bfloat16)
    slot_grad = jnp.dot(gate_grad, gate_w.T, preferred_element_type=jnp.float32)
    slot_grad = slot_grad + jnp.dot(up_grad, up_w.T, preferred_element_type=jnp.float32)
    return outputs, slot_grad.astype(jnp.bfloat16), down_grad


def reference(tokens, expert_ids, gates, cotangent, w_gate, w_up, w_down):
    one_hot = (expert_ids[:, :, None] == jnp.arange(EXPERTS, dtype=jnp.int32)[None, None, :]).astype(jnp.int32)
    per_device = one_hot.reshape(N_EXPERT, TOK_DEV * TOPK, EXPERTS)
    earlier = jnp.cumsum(per_device, axis=1) - per_device
    ranks = jnp.sum(earlier * per_device, axis=2).reshape(TOKENS, TOPK)
    source = (jnp.arange(TOKENS, dtype=jnp.int32) // TOK_DEV)[:, None]
    slot_ids = (expert_ids * (EXPERTS * CAP) + source * CAP + ranks).reshape(-1).astype(jnp.int32)
    total_slots = EXPERTS * EXPERTS * CAP
    spread_rows = jnp.repeat(tokens, TOPK, axis=0)
    sent_rows = jnp.zeros((total_slots, D), jnp.bfloat16).at[slot_ids].set(spread_rows)
    scaled = (gates[:, :, None] * cotangent.astype(jnp.float32)[:, None, :]).astype(jnp.bfloat16)
    sent_grads = jnp.zeros((total_slots, D), jnp.bfloat16).at[slot_ids].set(scaled.reshape(TOKENS * TOPK, D))
    outputs, input_grads, down_grads = lax.map(
        expert_pass,
        (sent_rows.reshape(EXPERTS, EXPERTS * CAP, D), sent_grads.reshape(EXPERTS, EXPERTS * CAP, D), w_gate, w_up, w_down))
    picked_out = outputs.reshape(total_slots, D)[slot_ids].astype(jnp.float32).reshape(TOKENS, TOPK, D)
    picked_grad = input_grads.reshape(total_slots, D)[slot_ids].astype(jnp.float32).reshape(TOKENS, TOPK, D)
    mixed = jnp.sum(gates[:, :, None] * picked_out, axis=1).astype(jnp.bfloat16)
    token_grads = jnp.sum(picked_grad, axis=1).astype(jnp.bfloat16)
    return mixed, token_grads, down_grads
```

```python
import functools

import jax
import jax.numpy as jnp
from jax import lax
from jax.experimental import pallas as pl
from jax.experimental.pallas import tpu as pltpu
from jax.sharding import PartitionSpec as P


def local(tokens, expert_ids, gates, cotangent, w_gate, w_up, w_down):
    tok_rows, top_count = expert_ids.shape
    col_span = tokens.shape[1]
    expert_count = lax.axis_size("expert")
    capacity = capacity_of(tok_rows, top_count, expert_count)
    slot_total = expert_count * capacity
    one_hot = (
        expert_ids[:, :, None] == jnp.arange(expert_count, dtype=jnp.int32)[None, None, :]
    ).astype(jnp.int32)
    one_hot = one_hot.reshape(tok_rows * top_count, expert_count)
    earlier = jnp.cumsum(one_hot, axis=0) - one_hot
    ranks = jnp.sum(earlier * one_hot, axis=1)
    slot_ids = expert_ids.reshape(-1) * capacity + ranks
    picker = (slot_ids[:, None] == jnp.arange(slot_total, dtype=jnp.int32)[None, :]).astype(
        jnp.float32
    )
    picker_rows = picker.reshape(tok_rows, top_count, slot_total)
    chooser = jnp.sum(picker_rows, axis=1)
    weigher = jnp.sum(picker_rows * gates[:, :, None], axis=1)
    sent_rows = jnp.dot(
        chooser.T.astype(jnp.bfloat16), tokens, preferred_element_type=jnp.float32
    ).astype(jnp.bfloat16)
    sent_grads = jnp.dot(
        weigher.T, cotangent.astype(jnp.float32), precision=lax.Precision.HIGHEST
    ).astype(jnp.bfloat16)
    routed_rows, routed_grads = (
        lax.all_to_all(sent_rows, "expert", split_axis=0, concat_axis=0, tiled=True),
        lax.all_to_all(sent_grads, "expert", split_axis=0, concat_axis=0, tiled=True),
    )
    gate_w = w_gate[0]
    up_w = w_up[0]
    down_w = w_down[0]
    grad_term = jnp.einsum("rc,hc->rh", routed_grads, down_w, preferred_element_type=jnp.float32)
    gate_term = jnp.dot(routed_rows, gate_w, preferred_element_type=jnp.float32)
    up_term = jnp.dot(routed_rows, up_w, preferred_element_type=jnp.float32)
    gate_pre, up_pre, hidden_grad = (
        lax.psum_scatter(
            gate_term.astype(jnp.bfloat16), "section", scatter_dimension=1, tiled=True
        ).astype(jnp.float32),
        lax.psum_scatter(
            up_term.astype(jnp.bfloat16), "section", scatter_dimension=1, tiled=True
        ).astype(jnp.float32),
        lax.psum_scatter(
            grad_term.astype(jnp.bfloat16), "section", scatter_dimension=1, tiled=True
        ).astype(jnp.float32),
    )
    sigmoid_val = jax.nn.sigmoid(gate_pre)
    activated = gate_pre * sigmoid_val
    hidden = (activated * up_pre).astype(jnp.bfloat16)
    gate_grad = (
        hidden_grad * up_pre * sigmoid_val * (1.0 + gate_pre * (1.0 - sigmoid_val))
    ).astype(jnp.bfloat16)
    up_grad = (hidden_grad * activated).astype(jnp.bfloat16)
    full_hidden, full_gate_grad, full_up_grad = (
        lax.all_gather(hidden, "section", axis=1, tiled=True),
        lax.all_gather(gate_grad, "section", axis=1, tiled=True),
        lax.all_gather(up_grad, "section", axis=1, tiled=True),
    )
    out_rows = jnp.dot(full_hidden, down_w, preferred_element_type=jnp.float32).astype(jnp.bfloat16)
    down_grad = jnp.einsum(
        "rh,rc->hc", full_hidden, routed_grads, preferred_element_type=jnp.float32
    ).astype(jnp.bfloat16)
    slot_grad = jnp.einsum("rh,ch->rc", full_gate_grad, gate_w, preferred_element_type=jnp.float32)
    slot_grad = (
        slot_grad + jnp.einsum("rh,ch->rc", full_up_grad, up_w, preferred_element_type=jnp.float32)
    ).astype(jnp.bfloat16)
    back_out, back_grad = (
        lax.all_to_all(out_rows, "expert", split_axis=0, concat_axis=0, tiled=True),
        lax.all_to_all(slot_grad, "expert", split_axis=0, concat_axis=0, tiled=True),
    )
    picked_out = jnp.dot(picker.astype(jnp.bfloat16), back_out, preferred_element_type=jnp.float32)
    picked_out = picked_out.reshape(tok_rows, top_count, col_span)
    mixed = jnp.sum(gates[:, :, None] * picked_out, axis=1).astype(jnp.bfloat16)
    token_grads = jnp.dot(
        chooser.astype(jnp.bfloat16), back_grad, preferred_element_type=jnp.float32
    ).astype(jnp.bfloat16)
    return (mixed, token_grads, down_grad[None])


MESH = pl.DeviceIdType.MESH
GROUPS = 4
ORDER = (0, 2, 1, 3)
NT = (((1,), (1,)), ((), ()))
TN = (((0,), (0,)), ((), ()))
F32 = jnp.float32
BF = jnp.bfloat16


def expert_kernel(
    n_exp, cap, ids_c, ids_r, gate_c, gate_r, tok, cot, wg_h, wu_h, wd_h,
    mixed_o, tgrad_o, dg_o,
    wg, wu, wd, send, recv, part, r1, s2, r2, act, hbuf, obuf, back, dgbuf,
    w_sem, d_ss, d_rs, s1_ss, s1_rs, s2_ss, s2_rs, gy_ss, gy_rs, gm_ss, gm_rs,
    gr_ss, gr_rs, b_ss, b_rs, loc_sem, o_sem,
):
    me_e = lax.axis_index("expert")
    me_s = lax.axis_index("section")
    span = n_exp // GROUPS
    my_g, my_x = me_e // span, me_e % span
    my_y, my_c = me_s // 2, me_s % 2
    oth_y, oth_c = 1 - my_y, 1 - my_c
    mate = my_y * 2 + oth_c
    ypart = oth_y * 2 + my_c
    rows = span * cap
    slots = n_exp * cap
    n_tok, cols = tok.shape
    quarter = part.shape[-1]
    topk = ids_c.shape[1]

    def group_of(c):
        return ((my_g // 2 + c // 2) % 2) * 2 + (my_g % 2 + c % 2) % 2

    def peers(c):
        return [group_of(c) * span + (my_x + i) % span for i in range(span)]

    loads = [
        pltpu.make_async_copy(a, b, w_sem.at[i])
        for i, (a, b) in enumerate(((wg_h, wg), (wu_h, wu), (wd_h, wd)))
    ]
    for load in loads:
        load.start()

    barrier = pltpu.get_barrier_semaphore()
    for i in range(1, n_exp):
        pl.semaphore_signal(
            barrier, inc=1, device_id=(me_s, (me_e + i) % n_exp), device_id_type=MESH
        )
    for s in (mate, ypart):
        pl.semaphore_signal(barrier, inc=1, device_id=(s, me_e), device_id_type=MESH)

    e_r = lax.broadcasted_iota(jnp.int32, (n_exp, n_tok), 0)
    hot_r = [(ids_r[k : k + 1, :] == e_r).astype(F32) for k in range(topk)]
    t0 = lax.broadcasted_iota(jnp.int32, (n_tok, n_tok), 0)
    t1 = lax.broadcasted_iota(jnp.int32, (n_tok, n_tok), 1)
    earlier_r = jnp.dot(
        sum(hot_r).astype(BF), (t0 < t1).astype(BF), preferred_element_type=F32
    )
    s_iota = lax.broadcasted_iota(jnp.int32, (slots, n_tok), 0)
    chooser = jnp.zeros((slots, n_tok), F32)
    gcol = jnp.zeros((slots, 1), F32)
    for k in range(topk):
        base = earlier_r + sum(hot_r[:k], jnp.zeros_like(earlier_r))
        slot_k = jnp.sum(hot_r[k] * (base + e_r.astype(F32) * cap), axis=0, keepdims=True)
        hit = (slot_k.astype(jnp.int32) == s_iota).astype(F32)
        chooser = chooser + hit
        gcol = gcol + jnp.sum(hit * gate_r[k : k + 1, :], axis=1, keepdims=True)
    chooser = chooser.astype(BF)
    picked = jnp.dot(chooser, tok[...], preferred_element_type=F32).astype(BF)
    send[:, 0] = picked.reshape(n_exp, cap, cols)
    picked = (jnp.dot(chooser, cot[...], preferred_element_type=F32) * gcol).astype(BF)
    send[:, 1] = picked.reshape(n_exp, cap, cols)

    pl.semaphore_wait(barrier, n_exp + 1)

    def dispatch(peer):
        return pltpu.make_async_remote_copy(
            src_ref=send.at[peer], dst_ref=recv.at[me_e], send_sem=d_ss.at[peer],
            recv_sem=d_rs.at[me_e], device_id=(me_s, peer), device_id_type=MESH,
        )

    def arrived(peer):
        return pltpu.make_async_remote_copy(
            src_ref=send.at[peer], dst_ref=recv.at[peer], send_sem=d_ss.at[peer],
            recv_sem=d_rs.at[peer], device_id=(me_s, peer), device_id_type=MESH,
        )

    def give(peer):
        return pltpu.make_async_remote_copy(
            src_ref=obuf.at[peer], dst_ref=back.at[me_e], send_sem=b_ss.at[peer],
            recv_sem=b_rs.at[me_e], device_id=(me_s, peer), device_id_type=MESH,
        )

    def given(peer):
        return pltpu.make_async_remote_copy(
            src_ref=obuf.at[peer], dst_ref=back.at[peer], send_sem=b_ss.at[peer],
            recv_sem=b_rs.at[peer], device_id=(me_s, peer), device_id_type=MESH,
        )

    def to_section(src, dst, ss, rs, s):
        return pltpu.make_async_remote_copy(
            src_ref=src, dst_ref=dst, send_sem=ss, recv_sem=rs,
            device_id=(s, me_e), device_id_type=MESH,
        )

    own = pltpu.make_async_copy(send.at[me_e], recv.at[me_e], loc_sem.at[0])
    own.start()
    for c in ORDER:
        for i, peer in enumerate(peers(c)):
            if c or i:
                dispatch(peer).start()
    for load in loads:
        load.wait()

    def rs1(c):
        return to_section(part.at[c, oth_c], r1.at[c], s1_ss.at[c], s1_rs.at[c], mate)

    def rs2(c):
        return to_section(s2.at[c], r2.at[c], s2_ss.at[c], s2_rs.at[c], ypart)

    def ag_y(c, y=None):
        mine = act.at[c, my_c, my_y if y is None else y]
        return to_section(mine, mine, gy_ss.at[c], gy_rs.at[c], ypart)

    def ag_m(c, core=None):
        mine = act.at[c, my_c if core is None else core, my_y]
        return to_section(mine, mine, gm_ss.at[c], gm_rs.at[c], mate)

    def ag_r(c, core=None):
        mine = act.at[c, my_c if core is None else core, oth_y]
        return to_section(mine, mine, gr_ss.at[c], gr_rs.at[c], mate)

    def stage_a(c):
        for i, peer in enumerate(peers(c)):
            if c or i:
                arrived(peer).wait_recv()
            else:
                own.wait()
        first = group_of(c) * span
        x = recv[pl.ds(first, span), 0].reshape(rows, cols)
        g = recv[pl.ds(first, span), 1].reshape(rows, cols)
        for q in range(4):
            at = slice(q * quarter, (q + 1) * quarter)
            part[c, q // 2, q % 2, 0] = jnp.dot(
                x, wg[:, at], preferred_element_type=F32).astype(BF)
            part[c, q // 2, q % 2, 1] = jnp.dot(
                x, wu[:, at], preferred_element_type=F32).astype(BF)
            part[c, q // 2, q % 2, 2] = lax.dot_general(
                g, wd[at, :], NT, preferred_element_type=F32).astype(BF)
        rs1(c).start()

    def stage_b(c):
        rs1(c).wait_recv()
        s2[c] = (part[c, my_c, oth_y].astype(F32) + r1[c, oth_y].astype(F32)).astype(BF)
        rs2(c).start()

    def stage_c(c):
        rs2(c).wait_recv()
        total = (
            part[c, my_c, my_y].astype(F32) + r1[c, my_y].astype(F32) + r2[c].astype(F32)
        )
        pre, up, hg = total[0], total[1], total[2]
        sig = jax.nn.sigmoid(pre)
        silu = pre * sig
        act[c, my_c, my_y, 0] = (silu * up).astype(BF)
        act[c, my_c, my_y, 1] = (hg * up * sig * (1.0 + pre * (1.0 - sig))).astype(BF)
        act[c, my_c, my_y, 2] = (hg * silu).astype(BF)
        ag_y(c).start()
        ag_m(c).start()

    def stage_d(c):
        ag_y(c, oth_y).wait_recv()
        ag_r(c).start()

    def stage_e(c):
        ag_m(c, oth_c).wait_recv()
        ag_r(c, oth_c).wait_recv()
        h, gg, ug = [
            jnp.concatenate([act[c, q // 2, q % 2, j] for q in range(4)], axis=1)
            for j in range(3)
        ]
        group = group_of(c)
        hbuf[group] = h
        first = group * span
        out = jnp.dot(h, wd[...], preferred_element_type=F32).astype(BF)
        obuf[pl.ds(first, span), 0] = out.reshape(span, cap, cols)
        sg = lax.dot_general(gg, wg[...], NT, preferred_element_type=F32)
        sg = (sg + lax.dot_general(ug, wu[...], NT, preferred_element_type=F32)).astype(BF)
        obuf[pl.ds(first, span), 1] = sg.reshape(span, cap, cols)
        for i, peer in enumerate(peers(c)):
            if c or i:
                give(peer).start()
            else:
                pltpu.make_async_copy(obuf.at[me_e], back.at[me_e], loc_sem.at[1]).start()

    c0, c1, c2, c3 = ORDER
    for stage, c in (
        (stage_a, c0), (stage_b, c0), (stage_c, c0), (stage_d, c0), (stage_e, c0),
        (stage_a, c1), (stage_b, c1), (stage_a, c2), (stage_c, c1), (stage_b, c2),
        (stage_d, c1), (stage_c, c2), (stage_e, c1), (stage_d, c2), (stage_a, c3),
        (stage_e, c2), (stage_b, c3), (stage_c, c3), (stage_d, c3), (stage_e, c3),
    ):
        stage(c)

    store = pltpu.make_async_copy(dgbuf, dg_o, o_sem)
    all_g = recv[:, 1].reshape(slots, cols)
    for q in range(4):
        at = slice(q * quarter, (q + 1) * quarter)
        hq = hbuf[:, :, at].reshape(slots, quarter)
        dgbuf[at, :] = lax.dot_general(hq, all_g, TN, preferred_element_type=F32).astype(BF)
    store.start()

    e_c = lax.broadcasted_iota(jnp.int32, (n_tok, n_exp), 1)
    hot_c = [(ids_c[:, k : k + 1] == e_c).astype(F32) for k in range(topk)]
    earlier_c = jnp.dot((t1 < t0).astype(BF), sum(hot_c).astype(BF), preferred_element_type=F32)
    l_iota = lax.broadcasted_iota(jnp.int32, (n_tok, slots), 1)
    picks = []
    for k in range(topk):
        base = earlier_c + sum(hot_c[:k], jnp.zeros_like(earlier_c))
        slot_k = jnp.sum(hot_c[k] * (base + e_c.astype(F32) * cap), axis=1, keepdims=True)
        picks.append((slot_k.astype(jnp.int32) == l_iota).astype(F32))

    for c in ORDER:
        for i, peer in enumerate(peers(c)):
            if c or i:
                given(peer).wait_recv()
            else:
                pltpu.make_async_copy(obuf.at[me_e], back.at[me_e], loc_sem.at[1]).wait()
    outs = back[:, 0].reshape(slots, cols)
    mixed = sum(
        gate_c[:, k : k + 1]
        * jnp.dot(picks[k].astype(BF), outs, preferred_element_type=F32)
        for k in range(topk)
    )
    mixed_o[...] = mixed.astype(BF)
    tgrad_o[...] = jnp.dot(
        sum(picks).astype(BF), back[:, 1].reshape(slots, cols), preferred_element_type=F32
    ).astype(BF)

    for c in ORDER:
        for i, peer in enumerate(peers(c)):
            if c or i:
                dispatch(peer).wait_send()
                give(peer).wait_send()
        for copy in (rs1(c), rs2(c), ag_y(c), ag_m(c), ag_r(c)):
            copy.wait_send()
    store.wait()


def fused(tokens, expert_ids, gates, cotangent, w_gate, w_up, w_down):
    n_tok, topk = expert_ids.shape
    cols = tokens.shape[1]
    hid = w_gate.shape[2]
    n_exp, n_sec = lax.axis_size("expert"), lax.axis_size("section")
    cap = capacity_of(n_tok, topk, n_exp)
    rows = n_exp // GROUPS * cap
    quarter = hid // n_sec
    vm = pl.BlockSpec(memory_space=pltpu.VMEM)
    hbm = pl.BlockSpec(memory_space=pl.ANY)
    dma = pltpu.SemaphoreType.DMA
    per = (GROUPS, 2, 2, 3, rows, quarter)
    mixed, tgrad, dg = pl.pallas_call(
        functools.partial(expert_kernel, n_exp, cap),
        out_shape=(
            jax.ShapeDtypeStruct((n_tok, cols), BF),
            jax.ShapeDtypeStruct((n_tok, cols), BF),
            jax.ShapeDtypeStruct((hid, cols), BF),
        ),
        in_specs=[vm] * 6 + [hbm] * 3,
        out_specs=(vm, vm, hbm),
        scratch_shapes=[
            pltpu.VMEM((cols, hid), BF),
            pltpu.VMEM((cols, hid), BF),
            pltpu.VMEM((hid, cols), BF),
            pltpu.VMEM((n_exp, 2, cap, cols), BF),
            pltpu.VMEM((n_exp, 2, cap, cols), BF),
            pltpu.VMEM(per, BF),
            pltpu.VMEM((GROUPS, 2, 3, rows, quarter), BF),
            pltpu.VMEM((GROUPS, 3, rows, quarter), BF),
            pltpu.VMEM((GROUPS, 3, rows, quarter), BF),
            pltpu.VMEM(per, BF),
            pltpu.VMEM((GROUPS, rows, hid), BF),
            pltpu.VMEM((n_exp, 2, cap, cols), BF),
            pltpu.VMEM((n_exp, 2, cap, cols), BF),
            pltpu.VMEM((hid, cols), BF),
            dma((3,)),
            dma((n_exp,)), dma((n_exp,)),
        ]
        + [dma((GROUPS,)) for _ in range(10)]
        + [dma((n_exp,)), dma((n_exp,)), dma((2,)), dma],
        compiler_params=pltpu.CompilerParams(
            collective_id=0, has_side_effects=True, vmem_limit_bytes=60 * 1024 * 1024
        ),
    )(
        expert_ids, expert_ids.T, gates, gates.T, tokens, cotangent,
        w_gate[0], w_up[0], w_down[0],
    )
    return mixed, tgrad, dg[None]


def capacity_of(tok_rows, top_count, expert_count):
    return min(tok_rows, max(2, 3 * tok_rows * top_count // (2 * expert_count)))


def layer(tokens, expert_ids, *rest):
    n_exp, n_sec = lax.axis_size("expert"), lax.axis_size("section")
    n_tok, topk = expert_ids.shape
    cap = capacity_of(n_tok, topk, n_exp)
    hid = rest[2].shape[2]
    tiles = (
        n_exp % GROUPS == 0 and n_sec == 4 and cap % 16 == 0 and n_tok % 128 == 0
        and tokens.shape[1] % 128 == 0 and hid % (n_sec * 128) == 0
    )
    return (fused if tiles else local)(tokens, expert_ids, *rest)


def solution(mesh):
    placed = (
        P("expert", "section"),
        P("expert", None),
        P("expert", None),
        P("expert", "section"),
        P("expert", "section", None),
        P("expert", "section", None),
        P("expert", None, "section"),
    )
    return jax.shard_map(
        layer,
        mesh=mesh,
        in_specs=placed,
        out_specs=(P("expert", "section"), P("expert", "section"), P("expert", None, "section")),
        check_vma=False,
    )
```

```python
import functools

import jax
import jax.numpy as jnp
from jax import lax
from jax.experimental import pallas as pl
from jax.experimental.pallas import tpu as pltpu
from jax.sharding import PartitionSpec as P


def local(tokens, expert_ids, gates, cotangent, w_gate, w_up, w_down):
    tok_rows, top_count = expert_ids.shape
    col_span = tokens.shape[1]
    expert_count = lax.axis_size("expert")
    capacity = capacity_of(tok_rows, top_count, expert_count)
    slot_total = expert_count * capacity
    one_hot = (
        expert_ids[:, :, None] == jnp.arange(expert_count, dtype=jnp.int32)[None, None, :]
    ).astype(jnp.int32)
    one_hot = one_hot.reshape(tok_rows * top_count, expert_count)
    earlier = jnp.cumsum(one_hot, axis=0) - one_hot
    ranks = jnp.sum(earlier * one_hot, axis=1)
    slot_ids = expert_ids.reshape(-1) * capacity + ranks
    picker = (slot_ids[:, None] == jnp.arange(slot_total, dtype=jnp.int32)[None, :]).astype(
        jnp.float32
    )
    picker_rows = picker.reshape(tok_rows, top_count, slot_total)
    chooser = jnp.sum(picker_rows, axis=1)
    weigher = jnp.sum(picker_rows * gates[:, :, None], axis=1)
    sent_rows = jnp.dot(
        chooser.T.astype(jnp.bfloat16), tokens, preferred_element_type=jnp.float32
    ).astype(jnp.bfloat16)
    sent_grads = jnp.dot(
        weigher.T, cotangent.astype(jnp.float32), precision=lax.Precision.HIGHEST
    ).astype(jnp.bfloat16)
    routed_rows, routed_grads = (
        lax.all_to_all(sent_rows, "expert", split_axis=0, concat_axis=0, tiled=True),
        lax.all_to_all(sent_grads, "expert", split_axis=0, concat_axis=0, tiled=True),
    )
    gate_w = w_gate[0]
    up_w = w_up[0]
    down_w = w_down[0]
    grad_term = jnp.einsum("rc,hc->rh", routed_grads, down_w, preferred_element_type=jnp.float32)
    gate_term = jnp.dot(routed_rows, gate_w, preferred_element_type=jnp.float32)
    up_term = jnp.dot(routed_rows, up_w, preferred_element_type=jnp.float32)
    gate_pre, up_pre, hidden_grad = (
        lax.psum_scatter(
            gate_term.astype(jnp.bfloat16), "section", scatter_dimension=1, tiled=True
        ).astype(jnp.float32),
        lax.psum_scatter(
            up_term.astype(jnp.bfloat16), "section", scatter_dimension=1, tiled=True
        ).astype(jnp.float32),
        lax.psum_scatter(
            grad_term.astype(jnp.bfloat16), "section", scatter_dimension=1, tiled=True
        ).astype(jnp.float32),
    )
    sigmoid_val = jax.nn.sigmoid(gate_pre)
    activated = gate_pre * sigmoid_val
    hidden = (activated * up_pre).astype(jnp.bfloat16)
    gate_grad = (
        hidden_grad * up_pre * sigmoid_val * (1.0 + gate_pre * (1.0 - sigmoid_val))
    ).astype(jnp.bfloat16)
    up_grad = (hidden_grad * activated).astype(jnp.bfloat16)
    full_hidden, full_gate_grad, full_up_grad = (
        lax.all_gather(hidden, "section", axis=1, tiled=True),
        lax.all_gather(gate_grad, "section", axis=1, tiled=True),
        lax.all_gather(up_grad, "section", axis=1, tiled=True),
    )
    out_rows = jnp.dot(full_hidden, down_w, preferred_element_type=jnp.float32).astype(jnp.bfloat16)
    down_grad = jnp.einsum(
        "rh,rc->hc", full_hidden, routed_grads, preferred_element_type=jnp.float32
    ).astype(jnp.bfloat16)
    slot_grad = jnp.einsum("rh,ch->rc", full_gate_grad, gate_w, preferred_element_type=jnp.float32)
    slot_grad = (
        slot_grad + jnp.einsum("rh,ch->rc", full_up_grad, up_w, preferred_element_type=jnp.float32)
    ).astype(jnp.bfloat16)
    back_out, back_grad = (
        lax.all_to_all(out_rows, "expert", split_axis=0, concat_axis=0, tiled=True),
        lax.all_to_all(slot_grad, "expert", split_axis=0, concat_axis=0, tiled=True),
    )
    picked_out = jnp.dot(picker.astype(jnp.bfloat16), back_out, preferred_element_type=jnp.float32)
    picked_out = picked_out.reshape(tok_rows, top_count, col_span)
    mixed = jnp.sum(gates[:, :, None] * picked_out, axis=1).astype(jnp.bfloat16)
    token_grads = jnp.dot(
        chooser.astype(jnp.bfloat16), back_grad, preferred_element_type=jnp.float32
    ).astype(jnp.bfloat16)
    return (mixed, token_grads, down_grad[None])


MESH = pl.DeviceIdType.MESH
GROUPS = 4
ORDER = (0, 2, 1, 3)
DISPATCH = (2, 0, 1, 3)
NT = (((1,), (1,)), ((), ()))
TN = (((0,), (0,)), ((), ()))
F32 = jnp.float32
BF = jnp.bfloat16


def expert_kernel(
    n_exp, cap, ids_r, gate_r, tok, cot, wg_h, wu_h, wd_h,
    back, dg_o,
    wg, wu, wd, send, recv, part, r1, s2, r2, act, hbuf, obuf, dgbuf,
    w_sem, d_ss, d_rs, s1_ss, s1_rs, s2_ss, s2_rs, gy_ss, gy_rs, gm_ss, gm_rs,
    gr_ss, gr_rs, b_ss, b_rs, loc_sem, o_sem,
):
    me_e = lax.axis_index("expert")
    me_s = lax.axis_index("section")
    span = n_exp // GROUPS
    my_g, my_x = me_e // span, me_e % span
    my_y, my_c = me_s // 2, me_s % 2
    oth_y, oth_c = 1 - my_y, 1 - my_c
    mate = my_y * 2 + oth_c
    ypart = oth_y * 2 + my_c
    rows = span * cap
    slots = n_exp * cap
    n_tok, cols = tok.shape
    quarter = part.shape[-1]
    topk = ids_r.shape[0]

    def group_of(c):
        return ((my_g // 2 + c // 2) % 2) * 2 + (my_g % 2 + c % 2) % 2

    def peers(c):
        return [group_of(c) * span + (my_x + i) % span for i in range(span)]

    loads = [
        pltpu.make_async_copy(a, b, w_sem.at[i])
        for i, (a, b) in enumerate(((wg_h, wg), (wu_h, wu), (wd_h, wd)))
    ]
    for load in loads:
        load.start()

    barrier = pltpu.get_barrier_semaphore()
    for i in range(1, n_exp):
        pl.semaphore_signal(
            barrier, inc=1, device_id=(me_s, (me_e + i) % n_exp), device_id_type=MESH
        )
    for s in (mate, ypart):
        pl.semaphore_signal(barrier, inc=1, device_id=(s, me_e), device_id_type=MESH)

    e_r = lax.broadcasted_iota(jnp.int32, (n_exp, n_tok), 0)
    hot_r = [(ids_r[k : k + 1, :] == e_r).astype(F32) for k in range(topk)]
    t0 = lax.broadcasted_iota(jnp.int32, (n_tok, n_tok), 0)
    t1 = lax.broadcasted_iota(jnp.int32, (n_tok, n_tok), 1)
    earlier_r = jnp.dot(
        sum(hot_r).astype(BF), (t0 < t1).astype(BF), preferred_element_type=F32
    )
    def dispatch(peer):
        return pltpu.make_async_remote_copy(
            src_ref=send.at[peer], dst_ref=recv.at[me_e], send_sem=d_ss.at[peer],
            recv_sem=d_rs.at[me_e], device_id=(me_s, peer), device_id_type=MESH,
        )

    def arrived(peer):
        return pltpu.make_async_remote_copy(
            src_ref=send.at[peer], dst_ref=recv.at[peer], send_sem=d_ss.at[peer],
            recv_sem=d_rs.at[peer], device_id=(me_s, peer), device_id_type=MESH,
        )

    def give(peer):
        return pltpu.make_async_remote_copy(
            src_ref=obuf.at[peer], dst_ref=back.at[me_e], send_sem=b_ss.at[peer],
            recv_sem=b_rs.at[me_e], device_id=(me_s, peer), device_id_type=MESH,
        )

    def given(peer):
        return pltpu.make_async_remote_copy(
            src_ref=obuf.at[peer], dst_ref=back.at[peer], send_sem=b_ss.at[peer],
            recv_sem=b_rs.at[peer], device_id=(me_s, peer), device_id_type=MESH,
        )

    def to_section(src, dst, ss, rs, s):
        return pltpu.make_async_remote_copy(
            src_ref=src, dst_ref=dst, send_sem=ss, recv_sem=rs,
            device_id=(s, me_e), device_id_type=MESH,
        )

    slot_r = []
    for k in range(topk):
        base = earlier_r + sum(hot_r[:k], jnp.zeros_like(earlier_r))
        slot_k = jnp.sum(hot_r[k] * (base + e_r.astype(F32) * cap), axis=0, keepdims=True)
        slot_r.append(slot_k.astype(jnp.int32))
    s_iota = lax.broadcasted_iota(jnp.int32, (rows, n_tok), 0)
    own = pltpu.make_async_copy(send.at[me_e], recv.at[me_e], loc_sem.at[0])
    for c in DISPATCH:
        first = group_of(c) * span
        chooser = jnp.zeros((rows, n_tok), F32)
        gcol = jnp.zeros((rows, 1), F32)
        for k in range(topk):
            hit = (slot_r[k] - first * cap == s_iota).astype(F32)
            chooser = chooser + hit
            gcol = gcol + jnp.sum(hit * gate_r[k : k + 1, :], axis=1, keepdims=True)
        chooser = chooser.astype(BF)
        picked = jnp.dot(chooser, tok[...], preferred_element_type=F32).astype(BF)
        send[pl.ds(first, span), 0] = picked.reshape(span, cap, cols)
        picked = (jnp.dot(chooser, cot[...], preferred_element_type=F32) * gcol).astype(BF)
        send[pl.ds(first, span), 1] = picked.reshape(span, cap, cols)
        if c == DISPATCH[0]:
            pl.semaphore_wait(barrier, n_exp + 1)
        for i, peer in enumerate(peers(c)):
            if c or i:
                dispatch(peer).start()
            else:
                own.start()
    for load in loads:
        load.wait()

    def rs1(c):
        return to_section(part.at[c, oth_c], r1.at[c], s1_ss.at[c], s1_rs.at[c], mate)

    def rs2(c):
        return to_section(s2.at[c], r2.at[c], s2_ss.at[c], s2_rs.at[c], ypart)

    def ag_y(c, y=None):
        mine = act.at[c, my_c, my_y if y is None else y]
        return to_section(mine, mine, gy_ss.at[c], gy_rs.at[c], ypart)

    def ag_m(c, core=None):
        mine = act.at[c, my_c if core is None else core, my_y]
        return to_section(mine, mine, gm_ss.at[c], gm_rs.at[c], mate)

    def ag_r(c, core=None):
        mine = act.at[c, my_c if core is None else core, oth_y]
        return to_section(mine, mine, gr_ss.at[c], gr_rs.at[c], mate)

    def stage_a(c):
        for i, peer in enumerate(peers(c)):
            if c or i:
                arrived(peer).wait_recv()
            else:
                own.wait()
        first = group_of(c) * span
        x = recv[pl.ds(first, span), 0].reshape(rows, cols)
        g = recv[pl.ds(first, span), 1].reshape(rows, cols)
        for q in range(4):
            at = slice(q * quarter, (q + 1) * quarter)
            part[c, q // 2, q % 2, 0] = jnp.dot(
                x, wg[:, at], preferred_element_type=F32).astype(BF)
            part[c, q // 2, q % 2, 1] = jnp.dot(
                x, wu[:, at], preferred_element_type=F32).astype(BF)
            part[c, q // 2, q % 2, 2] = lax.dot_general(
                g, wd[at, :], NT, preferred_element_type=F32).astype(BF)
        rs1(c).start()

    def stage_b(c):
        rs1(c).wait_recv()
        s2[c] = (part[c, my_c, oth_y].astype(F32) + r1[c, oth_y].astype(F32)).astype(BF)
        rs2(c).start()

    def stage_c(c):
        rs2(c).wait_recv()
        total = (
            part[c, my_c, my_y].astype(F32) + r1[c, my_y].astype(F32) + r2[c].astype(F32)
        )
        pre, up, hg = total[0], total[1], total[2]
        sig = jax.nn.sigmoid(pre)
        silu = pre * sig
        act[c, my_c, my_y, 0] = (silu * up).astype(BF)
        act[c, my_c, my_y, 1] = (hg * up * sig * (1.0 + pre * (1.0 - sig))).astype(BF)
        act[c, my_c, my_y, 2] = (hg * silu).astype(BF)
        ag_y(c).start()
        ag_m(c).start()

    def stage_d(c):
        ag_y(c, oth_y).wait_recv()
        ag_r(c).start()

    def stage_e(c):
        ag_m(c, oth_c).wait_recv()
        ag_r(c, oth_c).wait_recv()
        h, gg, ug = [
            jnp.concatenate([act[c, q // 2, q % 2, j] for q in range(4)], axis=1)
            for j in range(3)
        ]
        group = group_of(c)
        hbuf[group] = h
        first = group * span
        out = jnp.dot(h, wd[...], preferred_element_type=F32).astype(BF)
        obuf[pl.ds(first, span), 0] = out.reshape(span, cap, cols)
        sg = lax.dot_general(gg, wg[...], NT, preferred_element_type=F32)
        sg = (sg + lax.dot_general(ug, wu[...], NT, preferred_element_type=F32)).astype(BF)
        obuf[pl.ds(first, span), 1] = sg.reshape(span, cap, cols)
        for i, peer in enumerate(peers(c)):
            if c or i:
                give(peer).start()
            else:
                pltpu.make_async_copy(obuf.at[me_e], back.at[me_e], loc_sem.at[1]).start()

    c0, c1, c2, c3 = ORDER
    for stage, c in (
        (stage_a, c0), (stage_b, c0), (stage_c, c0), (stage_d, c0), (stage_e, c0),
        (stage_a, c1), (stage_b, c1), (stage_c, c1), (stage_d, c1), (stage_e, c1),
        (stage_a, c2), (stage_b, c2), (stage_a, c3), (stage_c, c2), (stage_b, c3),
        (stage_d, c2), (stage_c, c3), (stage_e, c2), (stage_d, c3), (stage_e, c3),
    ):
        stage(c)

    store = pltpu.make_async_copy(dgbuf, dg_o, o_sem)
    all_g = recv[:, 1].reshape(slots, cols)
    for q in range(4):
        at = slice(q * quarter, (q + 1) * quarter)
        hq = hbuf[:, :, at].reshape(slots, quarter)
        dgbuf[at, :] = lax.dot_general(hq, all_g, TN, preferred_element_type=F32).astype(BF)
    store.start()

    for c in ORDER:
        for i, peer in enumerate(peers(c)):
            if c or i:
                given(peer).wait_recv()
            else:
                pltpu.make_async_copy(obuf.at[me_e], back.at[me_e], loc_sem.at[1]).wait()
    for c in ORDER:
        for i, peer in enumerate(peers(c)):
            if c or i:
                dispatch(peer).wait_send()
                give(peer).wait_send()
        for copy in (rs1(c), rs2(c), ag_y(c), ag_m(c), ag_r(c)):
            copy.wait_send()
    store.wait()


def combine_kernel(n_exp, cap, ids_r, gate_r, back_h, dg_h, mixed_o, tgrad_o, dg_o, back, dg, sem):
    topk, n_tok = ids_r.shape
    hid, cols = dg.shape
    slots = n_exp * cap
    part = hid // GROUPS
    half = n_exp // 2
    gets = [
        pltpu.make_async_copy(
            back_h.at[pl.ds(i * half, half)], back.at[pl.ds(i * half, half)], sem.at[i]
        )
        for i in range(2)
    ]
    ins = [
        pltpu.make_async_copy(
            dg_h.at[pl.ds(i * part, part)], dg.at[pl.ds(i * part, part)], sem.at[2 + i]
        )
        for i in range(GROUPS)
    ]
    outs = [
        pltpu.make_async_copy(
            dg.at[pl.ds(i * part, part)], dg_o.at[pl.ds(i * part, part)], sem.at[2 + GROUPS + i]
        )
        for i in range(GROUPS)
    ]
    for get in gets + ins:
        get.start()
    t0 = lax.broadcasted_iota(jnp.int32, (n_tok, n_tok), 0)
    t1 = lax.broadcasted_iota(jnp.int32, (n_tok, n_tok), 1)
    eye = (t0 == t1).astype(F32)
    e_r = lax.broadcasted_iota(jnp.int32, (n_exp, n_tok), 0)
    hot = [(ids_r[k : k + 1, :] == e_r).astype(F32) for k in range(topk)]
    earlier = jnp.dot(sum(hot).astype(BF), (t0 < t1).astype(BF), preferred_element_type=F32)
    l_iota = lax.broadcasted_iota(jnp.int32, (n_tok, slots), 1)
    picks, weights = [], []
    for k in range(topk):
        base = earlier + sum(hot[:k], jnp.zeros_like(earlier))
        slot_k = jnp.sum(hot[k] * (base + e_r.astype(F32) * cap), axis=0, keepdims=True)
        column = jnp.sum(eye * slot_k, axis=1, keepdims=True).astype(jnp.int32)
        picks.append((column == l_iota).astype(F32))
        weights.append(jnp.sum(eye * gate_r[k : k + 1, :], axis=1, keepdims=True))
    for get in gets:
        get.wait()
    for i in range(GROUPS):
        ins[i].wait()
        outs[i].start()
    rows_out = back[:, 0].reshape(slots, cols)
    mixed = sum(
        weights[k] * jnp.dot(picks[k].astype(BF), rows_out, preferred_element_type=F32)
        for k in range(topk)
    )
    mixed_o[...] = mixed.astype(BF)
    tgrad_o[...] = jnp.dot(
        sum(picks).astype(BF), back[:, 1].reshape(slots, cols), preferred_element_type=F32
    ).astype(BF)
    for put in outs:
        put.wait()


def fused(tokens, expert_ids, gates, cotangent, w_gate, w_up, w_down):
    n_tok, topk = expert_ids.shape
    cols = tokens.shape[1]
    hid = w_gate.shape[2]
    n_exp, n_sec = lax.axis_size("expert"), lax.axis_size("section")
    cap = capacity_of(n_tok, topk, n_exp)
    rows = n_exp // GROUPS * cap
    quarter = hid // n_sec
    vm = pl.BlockSpec(memory_space=pltpu.VMEM)
    hbm = pl.BlockSpec(memory_space=pl.ANY)
    dma = pltpu.SemaphoreType.DMA
    per = (GROUPS, 2, 2, 3, rows, quarter)
    ids_r, gate_r = expert_ids.T, gates.T
    back, dg = pl.pallas_call(
        functools.partial(expert_kernel, n_exp, cap),
        out_shape=(
            jax.ShapeDtypeStruct((n_exp, 2, cap, cols), BF),
            jax.ShapeDtypeStruct((hid, cols), BF),
        ),
        in_specs=[vm] * 4 + [hbm] * 3,
        out_specs=(hbm, hbm),
        scratch_shapes=[
            pltpu.VMEM((cols, hid), BF),
            pltpu.VMEM((cols, hid), BF),
            pltpu.VMEM((hid, cols), BF),
            pltpu.VMEM((n_exp, 2, cap, cols), BF),
            pltpu.VMEM((n_exp, 2, cap, cols), BF),
            pltpu.VMEM(per, BF),
            pltpu.VMEM((GROUPS, 2, 3, rows, quarter), BF),
            pltpu.VMEM((GROUPS, 3, rows, quarter), BF),
            pltpu.VMEM((GROUPS, 3, rows, quarter), BF),
            pltpu.VMEM(per, BF),
            pltpu.VMEM((GROUPS, rows, hid), BF),
            pltpu.VMEM((n_exp, 2, cap, cols), BF),
            pltpu.VMEM((hid, cols), BF),
            dma((3,)),
            dma((n_exp,)), dma((n_exp,)),
        ]
        + [dma((GROUPS,)) for _ in range(10)]
        + [dma((n_exp,)), dma((n_exp,)), dma((2,)), dma],
        compiler_params=pltpu.CompilerParams(
            collective_id=0, has_side_effects=True, vmem_limit_bytes=60 * 1024 * 1024
        ),
    )(ids_r, gate_r, tokens, cotangent, w_gate[0], w_up[0], w_down[0])
    mixed, tgrad, dg = pl.pallas_call(
        functools.partial(combine_kernel, n_exp, cap),
        out_shape=(
            jax.ShapeDtypeStruct((n_tok, cols), BF),
            jax.ShapeDtypeStruct((n_tok, cols), BF),
            jax.ShapeDtypeStruct((hid, cols), BF),
        ),
        in_specs=[vm] * 2 + [hbm] * 2,
        out_specs=(vm, vm, hbm),
        scratch_shapes=[
            pltpu.VMEM((n_exp, 2, cap, cols), BF),
            pltpu.VMEM((hid, cols), BF),
            dma((2 + 2 * GROUPS,)),
        ],
        compiler_params=pltpu.CompilerParams(vmem_limit_bytes=32 * 1024 * 1024),
    )(ids_r, gate_r, back, dg)
    return mixed, tgrad, dg[None]


def capacity_of(tok_rows, top_count, expert_count):
    return min(tok_rows, max(2, 3 * tok_rows * top_count // (2 * expert_count)))


def layer(tokens, expert_ids, *rest):
    n_exp, n_sec = lax.axis_size("expert"), lax.axis_size("section")
    n_tok, topk = expert_ids.shape
    cap = capacity_of(n_tok, topk, n_exp)
    hid = rest[2].shape[2]
    tiles = (
        n_exp % GROUPS == 0 and n_sec == 4 and cap % 16 == 0 and n_tok % 128 == 0
        and tokens.shape[1] % 128 == 0 and hid % (n_sec * 128) == 0
    )
    return (fused if tiles else local)(tokens, expert_ids, *rest)


def solution(mesh):
    placed = (
        P("expert", "section"),
        P("expert", None),
        P("expert", None),
        P("expert", "section"),
        P("expert", "section", None),
        P("expert", "section", None),
        P("expert", None, "section"),
    )
    return jax.shard_map(
        layer,
        mesh=mesh,
        in_specs=placed,
        out_specs=(P("expert", "section"), P("expert", "section"), P("expert", None, "section")),
        check_vma=False,
    )
```

```python
import functools

import jax
import jax.numpy as jnp
from jax import lax
from jax.experimental import pallas as pl
from jax.experimental.pallas import tpu as pltpu
from jax.sharding import PartitionSpec as P


def local(tokens, expert_ids, gates, cotangent, w_gate, w_up, w_down):
    tok_rows, top_count = expert_ids.shape
    col_span = tokens.shape[1]
    expert_count = lax.axis_size("expert")
    capacity = capacity_of(tok_rows, top_count, expert_count)
    slot_total = expert_count * capacity
    one_hot = (
        expert_ids[:, :, None] == jnp.arange(expert_count, dtype=jnp.int32)[None, None, :]
    ).astype(jnp.int32)
    one_hot = one_hot.reshape(tok_rows * top_count, expert_count)
    earlier = jnp.cumsum(one_hot, axis=0) - one_hot
    ranks = jnp.sum(earlier * one_hot, axis=1)
    slot_ids = expert_ids.reshape(-1) * capacity + ranks
    picker = (slot_ids[:, None] == jnp.arange(slot_total, dtype=jnp.int32)[None, :]).astype(
        jnp.float32
    )
    picker_rows = picker.reshape(tok_rows, top_count, slot_total)
    chooser = jnp.sum(picker_rows, axis=1)
    weigher = jnp.sum(picker_rows * gates[:, :, None], axis=1)
    sent_rows = jnp.dot(
        chooser.T.astype(jnp.bfloat16), tokens, preferred_element_type=jnp.float32
    ).astype(jnp.bfloat16)
    sent_grads = jnp.dot(
        weigher.T, cotangent.astype(jnp.float32), precision=lax.Precision.HIGHEST
    ).astype(jnp.bfloat16)
    routed_rows, routed_grads = (
        lax.all_to_all(sent_rows, "expert", split_axis=0, concat_axis=0, tiled=True),
        lax.all_to_all(sent_grads, "expert", split_axis=0, concat_axis=0, tiled=True),
    )
    gate_w = w_gate[0]
    up_w = w_up[0]
    down_w = w_down[0]
    grad_term = jnp.einsum("rc,hc->rh", routed_grads, down_w, preferred_element_type=jnp.float32)
    gate_term = jnp.dot(routed_rows, gate_w, preferred_element_type=jnp.float32)
    up_term = jnp.dot(routed_rows, up_w, preferred_element_type=jnp.float32)
    gate_pre, up_pre, hidden_grad = (
        lax.psum_scatter(
            gate_term.astype(jnp.bfloat16), "section", scatter_dimension=1, tiled=True
        ).astype(jnp.float32),
        lax.psum_scatter(
            up_term.astype(jnp.bfloat16), "section", scatter_dimension=1, tiled=True
        ).astype(jnp.float32),
        lax.psum_scatter(
            grad_term.astype(jnp.bfloat16), "section", scatter_dimension=1, tiled=True
        ).astype(jnp.float32),
    )
    sigmoid_val = jax.nn.sigmoid(gate_pre)
    activated = gate_pre * sigmoid_val
    hidden = (activated * up_pre).astype(jnp.bfloat16)
    gate_grad = (
        hidden_grad * up_pre * sigmoid_val * (1.0 + gate_pre * (1.0 - sigmoid_val))
    ).astype(jnp.bfloat16)
    up_grad = (hidden_grad * activated).astype(jnp.bfloat16)
    full_hidden, full_gate_grad, full_up_grad = (
        lax.all_gather(hidden, "section", axis=1, tiled=True),
        lax.all_gather(gate_grad, "section", axis=1, tiled=True),
        lax.all_gather(up_grad, "section", axis=1, tiled=True),
    )
    out_rows = jnp.dot(full_hidden, down_w, preferred_element_type=jnp.float32).astype(jnp.bfloat16)
    down_grad = jnp.einsum(
        "rh,rc->hc", full_hidden, routed_grads, preferred_element_type=jnp.float32
    ).astype(jnp.bfloat16)
    slot_grad = jnp.einsum("rh,ch->rc", full_gate_grad, gate_w, preferred_element_type=jnp.float32)
    slot_grad = (
        slot_grad + jnp.einsum("rh,ch->rc", full_up_grad, up_w, preferred_element_type=jnp.float32)
    ).astype(jnp.bfloat16)
    back_out, back_grad = (
        lax.all_to_all(out_rows, "expert", split_axis=0, concat_axis=0, tiled=True),
        lax.all_to_all(slot_grad, "expert", split_axis=0, concat_axis=0, tiled=True),
    )
    picked_out = jnp.dot(picker.astype(jnp.bfloat16), back_out, preferred_element_type=jnp.float32)
    picked_out = picked_out.reshape(tok_rows, top_count, col_span)
    mixed = jnp.sum(gates[:, :, None] * picked_out, axis=1).astype(jnp.bfloat16)
    token_grads = jnp.dot(
        chooser.astype(jnp.bfloat16), back_grad, preferred_element_type=jnp.float32
    ).astype(jnp.bfloat16)
    return (mixed, token_grads, down_grad[None])


MESH = pl.DeviceIdType.MESH
GROUPS = 4
ORDER = (0, 2, 1, 3)
DISPATCH = (2, 0, 1, 3)
STEPS = (
    "A0", "B0", "A2", "B2", "C0", "C2", "A3", "D0", "B3", "D2",
    "E2", "E0", "C3", "A1", "D3", "A4", "B1", "E3", "B4", "A5",
    "C4", "B5", "C1", "D4", "C5", "E4", "D1", "D5", "E1", "E5",
)
NT = (((1,), (1,)), ((), ()))
TN = (((0,), (0,)), ((), ()))
F32 = jnp.float32
BF = jnp.bfloat16


def expert_kernel(
    n_exp, cap, ids_r, gate_r, tok, cot, wg_h, wu_h, wd_h,
    back, dg_o,
    wg, wu, wd, send, recv, part, r1, s2, r2, act, hbuf, obuf, dgbuf,
    w_sem, d_ss, d_rs, s1_ss, s1_rs, s2_ss, s2_rs, gy_ss, gy_rs, gm_ss, gm_rs,
    gr_ss, gr_rs, b_ss, b_rs, loc_sem, o_sem,
):
    me_e = lax.axis_index("expert")
    me_s = lax.axis_index("section")
    span = n_exp // GROUPS
    my_g, my_x = me_e // span, me_e % span
    my_y, my_c = me_s // 2, me_s % 2
    oth_y, oth_c = 1 - my_y, 1 - my_c
    mate = my_y * 2 + oth_c
    ypart = oth_y * 2 + my_c
    rows = span * cap
    slots = n_exp * cap
    n_tok, cols = tok.shape
    quarter = part.shape[-1]
    topk = ids_r.shape[0]

    def group_of(c):
        return ((my_g // 2 + c // 2) % 2) * 2 + (my_g % 2 + c % 2) % 2

    def peers(c):
        return [group_of(c) * span + (my_x + i) % span for i in range(span)]

    loads = [
        pltpu.make_async_copy(a, b, w_sem.at[i])
        for i, (a, b) in enumerate(((wg_h, wg), (wu_h, wu), (wd_h, wd)))
    ]
    for load in loads:
        load.start()

    barrier = pltpu.get_barrier_semaphore()
    for i in range(1, n_exp):
        pl.semaphore_signal(
            barrier, inc=1, device_id=(me_s, (me_e + i) % n_exp), device_id_type=MESH
        )
    for s in (mate, ypart):
        pl.semaphore_signal(barrier, inc=1, device_id=(s, me_e), device_id_type=MESH)

    e_r = lax.broadcasted_iota(jnp.int32, (n_exp, n_tok), 0)
    hot_r = [(ids_r[k : k + 1, :] == e_r).astype(F32) for k in range(topk)]
    t0 = lax.broadcasted_iota(jnp.int32, (n_tok, n_tok), 0)
    t1 = lax.broadcasted_iota(jnp.int32, (n_tok, n_tok), 1)
    earlier_r = jnp.dot(
        sum(hot_r).astype(BF), (t0 < t1).astype(BF), preferred_element_type=F32
    )
    def dispatch(peer):
        return pltpu.make_async_remote_copy(
            src_ref=send.at[peer], dst_ref=recv.at[me_e], send_sem=d_ss.at[peer],
            recv_sem=d_rs.at[me_e], device_id=(me_s, peer), device_id_type=MESH,
        )

    def arrived(peer):
        return pltpu.make_async_remote_copy(
            src_ref=send.at[peer], dst_ref=recv.at[peer], send_sem=d_ss.at[peer],
            recv_sem=d_rs.at[peer], device_id=(me_s, peer), device_id_type=MESH,
        )

    def give(peer):
        return pltpu.make_async_remote_copy(
            src_ref=obuf.at[peer], dst_ref=back.at[me_e], send_sem=b_ss.at[peer],
            recv_sem=b_rs.at[me_e], device_id=(me_s, peer), device_id_type=MESH,
        )

    def given(peer):
        return pltpu.make_async_remote_copy(
            src_ref=obuf.at[peer], dst_ref=back.at[peer], send_sem=b_ss.at[peer],
            recv_sem=b_rs.at[peer], device_id=(me_s, peer), device_id_type=MESH,
        )

    def to_section(src, dst, ss, rs, s):
        return pltpu.make_async_remote_copy(
            src_ref=src, dst_ref=dst, send_sem=ss, recv_sem=rs,
            device_id=(s, me_e), device_id_type=MESH,
        )

    slot_r = []
    for k in range(topk):
        base = earlier_r + sum(hot_r[:k], jnp.zeros_like(earlier_r))
        slot_k = jnp.sum(hot_r[k] * (base + e_r.astype(F32) * cap), axis=0, keepdims=True)
        slot_r.append(slot_k.astype(jnp.int32))
    s_iota = lax.broadcasted_iota(jnp.int32, (rows, n_tok), 0)
    own = pltpu.make_async_copy(send.at[me_e], recv.at[me_e], loc_sem.at[0])
    for c in DISPATCH:
        first = group_of(c) * span
        chooser = jnp.zeros((rows, n_tok), F32)
        gcol = jnp.zeros((rows, 1), F32)
        for k in range(topk):
            hit = (slot_r[k] - first * cap == s_iota).astype(F32)
            chooser = chooser + hit
            gcol = gcol + jnp.sum(hit * gate_r[k : k + 1, :], axis=1, keepdims=True)
        chooser = chooser.astype(BF)
        picked = jnp.dot(chooser, tok[...], preferred_element_type=F32).astype(BF)
        send[pl.ds(first, span), 0] = picked.reshape(span, cap, cols)
        picked = (jnp.dot(chooser, cot[...], preferred_element_type=F32) * gcol).astype(BF)
        send[pl.ds(first, span), 1] = picked.reshape(span, cap, cols)
        if c == DISPATCH[0]:
            pl.semaphore_wait(barrier, n_exp + 1)
        for i, peer in enumerate(peers(c)):
            if c or i:
                dispatch(peer).start()
            else:
                own.start()
    for load in loads:
        load.wait()

    def blocks(ch):
        c, i, n = ch
        return pl.ds(c * span + i, n)

    def first_of(ch):
        c, i, n = ch
        return group_of(c) * span + (0 if n == span else (my_x + i) % span)

    def members(ch):
        c, i, n = ch
        return [(c == 0 and j == 0, peers(c)[j]) for j in range(i, i + n)]

    def sem_of(ch):
        return ch[0] * span + ch[1]

    def rs1(ch):
        b, k = blocks(ch), sem_of(ch)
        return to_section(part.at[b, oth_c], r1.at[b], s1_ss.at[k], s1_rs.at[k], mate)

    def rs2(ch):
        b, k = blocks(ch), sem_of(ch)
        return to_section(s2.at[b], r2.at[b], s2_ss.at[k], s2_rs.at[k], ypart)

    def ag_y(ch, y=None):
        k = sem_of(ch)
        mine = act.at[blocks(ch), my_c, my_y if y is None else y]
        return to_section(mine, mine, gy_ss.at[k], gy_rs.at[k], ypart)

    def ag_m(ch, core=None):
        k = sem_of(ch)
        mine = act.at[blocks(ch), my_c if core is None else core, my_y]
        return to_section(mine, mine, gm_ss.at[k], gm_rs.at[k], mate)

    def ag_r(ch, core=None):
        k = sem_of(ch)
        mine = act.at[blocks(ch), my_c if core is None else core, oth_y]
        return to_section(mine, mine, gr_ss.at[k], gr_rs.at[k], mate)

    def stage_a(ch):
        n = ch[2]
        for here, peer in members(ch):
            if here:
                own.wait()
            else:
                arrived(peer).wait_recv()
        first = first_of(ch)
        x = recv[pl.ds(first, n), 0].reshape(n * cap, cols)
        g = recv[pl.ds(first, n), 1].reshape(n * cap, cols)
        for q in range(4):
            at = slice(q * quarter, (q + 1) * quarter)
            terms = (
                jnp.dot(x, wg[:, at], preferred_element_type=F32),
                jnp.dot(x, wu[:, at], preferred_element_type=F32),
                lax.dot_general(g, wd[at, :], NT, preferred_element_type=F32),
            )
            for j in range(3):
                part[blocks(ch), q // 2, q % 2, j] = (
                    terms[j].astype(BF).reshape(n, cap, quarter)
                )
        rs1(ch).start()

    def stage_b(ch):
        b = blocks(ch)
        rs1(ch).wait_recv()
        s2[b] = (part[b, my_c, oth_y].astype(F32) + r1[b, oth_y].astype(F32)).astype(BF)
        rs2(ch).start()

    def stage_c(ch):
        b = blocks(ch)
        rs2(ch).wait_recv()

        def total(j):
            return (
                part[b, my_c, my_y, j].astype(F32) + r1[b, my_y, j].astype(F32)
                + r2[b, j].astype(F32)
            )

        pre, up, hg = total(0), total(1), total(2)
        sig = jax.nn.sigmoid(pre)
        silu = pre * sig
        act[b, my_c, my_y, 0] = (silu * up).astype(BF)
        act[b, my_c, my_y, 1] = (hg * up * sig * (1.0 + pre * (1.0 - sig))).astype(BF)
        act[b, my_c, my_y, 2] = (hg * silu).astype(BF)
        ag_y(ch).start()
        ag_m(ch).start()

    def stage_d(ch):
        ag_y(ch, oth_y).wait_recv()
        ag_r(ch).start()

    def stage_e(ch):
        n = ch[2]
        ag_m(ch, oth_c).wait_recv()
        ag_r(ch, oth_c).wait_recv()
        h, gg, ug = [
            jnp.concatenate(
                [
                    act[blocks(ch), q // 2, q % 2, j].reshape(n * cap, quarter)
                    for q in range(4)
                ],
                axis=1,
            )
            for j in range(3)
        ]
        first = first_of(ch)
        hbuf[pl.ds(first, n)] = h.reshape(n, cap, 4 * quarter)
        out = jnp.dot(h, wd[...], preferred_element_type=F32).astype(BF)
        obuf[pl.ds(first, n), 0] = out.reshape(n, cap, cols)
        sg = lax.dot_general(gg, wg[...], NT, preferred_element_type=F32)
        sg = (sg + lax.dot_general(ug, wu[...], NT, preferred_element_type=F32)).astype(BF)
        obuf[pl.ds(first, n), 1] = sg.reshape(n, cap, cols)
        for here, peer in members(ch):
            if here:
                pltpu.make_async_copy(obuf.at[me_e], back.at[me_e], loc_sem.at[1]).start()
            else:
                give(peer).start()

    stages = {"A": stage_a, "B": stage_b, "C": stage_c, "D": stage_d, "E": stage_e}
    near = {"0": (0, 0, span), "1": (1, 0, span)}
    half = span // 2
    far = {
        "2": (2, 0, half), "3": (2, half, half), "4": (3, 0, half), "5": (3, half, half)
    }
    chunks = {**near, **far}
    for step in STEPS:
        stages[step[0]](chunks[step[1]])

    store = pltpu.make_async_copy(dgbuf, dg_o, o_sem)
    all_g = recv[:, 1].reshape(slots, cols)
    for q in range(4):
        at = slice(q * quarter, (q + 1) * quarter)
        hq = hbuf[:, :, at].reshape(slots, quarter)
        dgbuf[at, :] = lax.dot_general(hq, all_g, TN, preferred_element_type=F32).astype(BF)
    store.start()

    for c in ORDER:
        for i, peer in enumerate(peers(c)):
            if c or i:
                given(peer).wait_recv()
            else:
                pltpu.make_async_copy(obuf.at[me_e], back.at[me_e], loc_sem.at[1]).wait()
    for c in ORDER:
        for i, peer in enumerate(peers(c)):
            if c or i:
                dispatch(peer).wait_send()
                give(peer).wait_send()
    for ch in chunks.values():
        for copy in (rs1(ch), rs2(ch), ag_y(ch), ag_m(ch), ag_r(ch)):
            copy.wait_send()
    store.wait()


def combine_kernel(n_exp, cap, ids_r, gate_r, back_h, dg_h, mixed_o, tgrad_o, dg_o, back, dg, sem):
    topk, n_tok = ids_r.shape
    hid, cols = dg.shape
    slots = n_exp * cap
    part = hid // GROUPS
    half = n_exp // 2
    gets = [
        pltpu.make_async_copy(
            back_h.at[pl.ds(i * half, half)], back.at[pl.ds(i * half, half)], sem.at[i]
        )
        for i in range(2)
    ]
    ins = [
        pltpu.make_async_copy(
            dg_h.at[pl.ds(i * part, part)], dg.at[pl.ds(i * part, part)], sem.at[2 + i]
        )
        for i in range(GROUPS)
    ]
    outs = [
        pltpu.make_async_copy(
            dg.at[pl.ds(i * part, part)], dg_o.at[pl.ds(i * part, part)], sem.at[2 + GROUPS + i]
        )
        for i in range(GROUPS)
    ]
    for get in gets + ins:
        get.start()
    t0 = lax.broadcasted_iota(jnp.int32, (n_tok, n_tok), 0)
    t1 = lax.broadcasted_iota(jnp.int32, (n_tok, n_tok), 1)
    eye = (t0 == t1).astype(F32)
    e_r = lax.broadcasted_iota(jnp.int32, (n_exp, n_tok), 0)
    hot = [(ids_r[k : k + 1, :] == e_r).astype(F32) for k in range(topk)]
    earlier = jnp.dot(sum(hot).astype(BF), (t0 < t1).astype(BF), preferred_element_type=F32)
    l_iota = lax.broadcasted_iota(jnp.int32, (n_tok, slots), 1)
    picks, weights = [], []
    for k in range(topk):
        base = earlier + sum(hot[:k], jnp.zeros_like(earlier))
        slot_k = jnp.sum(hot[k] * (base + e_r.astype(F32) * cap), axis=0, keepdims=True)
        column = jnp.sum(eye * slot_k, axis=1, keepdims=True).astype(jnp.int32)
        picks.append((column == l_iota).astype(F32))
        weights.append(jnp.sum(eye * gate_r[k : k + 1, :], axis=1, keepdims=True))
    for get in gets:
        get.wait()
    for i in range(GROUPS):
        ins[i].wait()
        outs[i].start()
    rows_out = back[:, 0].reshape(slots, cols)
    mixed = sum(
        weights[k] * jnp.dot(picks[k].astype(BF), rows_out, preferred_element_type=F32)
        for k in range(topk)
    )
    mixed_o[...] = mixed.astype(BF)
    tgrad_o[...] = jnp.dot(
        sum(picks).astype(BF), back[:, 1].reshape(slots, cols), preferred_element_type=F32
    ).astype(BF)
    for put in outs:
        put.wait()


def fused(tokens, expert_ids, gates, cotangent, w_gate, w_up, w_down):
    n_tok, topk = expert_ids.shape
    cols = tokens.shape[1]
    hid = w_gate.shape[2]
    n_exp, n_sec = lax.axis_size("expert"), lax.axis_size("section")
    cap = capacity_of(n_tok, topk, n_exp)
    quarter = hid // n_sec
    vm = pl.BlockSpec(memory_space=pltpu.VMEM)
    hbm = pl.BlockSpec(memory_space=pl.ANY)
    dma = pltpu.SemaphoreType.DMA
    per = (n_exp, 2, 2, 3, cap, quarter)
    ids_r, gate_r = expert_ids.T, gates.T
    back, dg = pl.pallas_call(
        functools.partial(expert_kernel, n_exp, cap),
        out_shape=(
            jax.ShapeDtypeStruct((n_exp, 2, cap, cols), BF),
            jax.ShapeDtypeStruct((hid, cols), BF),
        ),
        in_specs=[vm] * 4 + [hbm] * 3,
        out_specs=(hbm, hbm),
        scratch_shapes=[
            pltpu.VMEM((cols, hid), BF),
            pltpu.VMEM((cols, hid), BF),
            pltpu.VMEM((hid, cols), BF),
            pltpu.VMEM((n_exp, 2, cap, cols), BF),
            pltpu.VMEM((n_exp, 2, cap, cols), BF),
            pltpu.VMEM(per, BF),
            pltpu.VMEM((n_exp, 2, 3, cap, quarter), BF),
            pltpu.VMEM((n_exp, 3, cap, quarter), BF),
            pltpu.VMEM((n_exp, 3, cap, quarter), BF),
            pltpu.VMEM(per, BF),
            pltpu.VMEM((n_exp, cap, hid), BF),
            pltpu.VMEM((n_exp, 2, cap, cols), BF),
            pltpu.VMEM((hid, cols), BF),
            dma((3,)),
            dma((n_exp,)), dma((n_exp,)),
        ]
        + [dma((n_exp,)) for _ in range(10)]
        + [dma((n_exp,)), dma((n_exp,)), dma((2,)), dma],
        compiler_params=pltpu.CompilerParams(
            collective_id=0, has_side_effects=True, vmem_limit_bytes=60 * 1024 * 1024
        ),
    )(ids_r, gate_r, tokens, cotangent, w_gate[0], w_up[0], w_down[0])
    mixed, tgrad, dg = pl.pallas_call(
        functools.partial(combine_kernel, n_exp, cap),
        out_shape=(
            jax.ShapeDtypeStruct((n_tok, cols), BF),
            jax.ShapeDtypeStruct((n_tok, cols), BF),
            jax.ShapeDtypeStruct((hid, cols), BF),
        ),
        in_specs=[vm] * 2 + [hbm] * 2,
        out_specs=(vm, vm, hbm),
        scratch_shapes=[
            pltpu.VMEM((n_exp, 2, cap, cols), BF),
            pltpu.VMEM((hid, cols), BF),
            dma((2 + 2 * GROUPS,)),
        ],
        compiler_params=pltpu.CompilerParams(vmem_limit_bytes=60 * 1024 * 1024),
    )(ids_r, gate_r, back, dg)
    return mixed, tgrad, dg[None]


def capacity_of(tok_rows, top_count, expert_count):
    return min(tok_rows, max(2, 3 * tok_rows * top_count // (2 * expert_count)))


def layer(tokens, expert_ids, *rest):
    n_exp, n_sec = lax.axis_size("expert"), lax.axis_size("section")
    n_tok, topk = expert_ids.shape
    cap = capacity_of(n_tok, topk, n_exp)
    hid = rest[2].shape[2]
    tiles = (
        n_exp == 2 * GROUPS and n_sec == 4 and cap % 16 == 0 and n_tok % 128 == 0
        and tokens.shape[1] % 128 == 0 and hid % (n_sec * 128) == 0
    )
    return (fused if tiles else local)(tokens, expert_ids, *rest)


def solution(mesh):
    placed = (
        P("expert", "section"),
        P("expert", None),
        P("expert", None),
        P("expert", "section"),
        P("expert", "section", None),
        P("expert", "section", None),
        P("expert", None, "section"),
    )
    return jax.shard_map(
        layer,
        mesh=mesh,
        in_specs=placed,
        out_specs=(P("expert", "section"), P("expert", "section"), P("expert", None, "section")),
        check_vma=False,
    )
```

```python
import functools

import jax
import jax.numpy as jnp
from jax import lax
from jax.experimental import pallas as pl
from jax.experimental.pallas import tpu as pltpu
from jax.sharding import PartitionSpec as P


def local(tokens, expert_ids, gates, cotangent, w_gate, w_up, w_down):
    tok_rows, top_count = expert_ids.shape
    col_span = tokens.shape[1]
    expert_count = lax.axis_size("expert")
    capacity = capacity_of(tok_rows, top_count, expert_count)
    slot_total = expert_count * capacity
    one_hot = (
        expert_ids[:, :, None] == jnp.arange(expert_count, dtype=jnp.int32)[None, None, :]
    ).astype(jnp.int32)
    one_hot = one_hot.reshape(tok_rows * top_count, expert_count)
    earlier = jnp.cumsum(one_hot, axis=0) - one_hot
    ranks = jnp.sum(earlier * one_hot, axis=1)
    slot_ids = expert_ids.reshape(-1) * capacity + ranks
    picker = (slot_ids[:, None] == jnp.arange(slot_total, dtype=jnp.int32)[None, :]).astype(
        jnp.float32
    )
    picker_rows = picker.reshape(tok_rows, top_count, slot_total)
    chooser = jnp.sum(picker_rows, axis=1)
    weigher = jnp.sum(picker_rows * gates[:, :, None], axis=1)
    sent_rows = jnp.dot(
        chooser.T.astype(jnp.bfloat16), tokens, preferred_element_type=jnp.float32
    ).astype(jnp.bfloat16)
    sent_grads = jnp.dot(
        weigher.T, cotangent.astype(jnp.float32), precision=lax.Precision.HIGHEST
    ).astype(jnp.bfloat16)
    routed_rows, routed_grads = (
        lax.all_to_all(sent_rows, "expert", split_axis=0, concat_axis=0, tiled=True),
        lax.all_to_all(sent_grads, "expert", split_axis=0, concat_axis=0, tiled=True),
    )
    gate_w = w_gate[0]
    up_w = w_up[0]
    down_w = w_down[0]
    grad_term = jnp.einsum("rc,hc->rh", routed_grads, down_w, preferred_element_type=jnp.float32)
    gate_term = jnp.dot(routed_rows, gate_w, preferred_element_type=jnp.float32)
    up_term = jnp.dot(routed_rows, up_w, preferred_element_type=jnp.float32)
    gate_pre, up_pre, hidden_grad = (
        lax.psum_scatter(
            gate_term.astype(jnp.bfloat16), "section", scatter_dimension=1, tiled=True
        ).astype(jnp.float32),
        lax.psum_scatter(
            up_term.astype(jnp.bfloat16), "section", scatter_dimension=1, tiled=True
        ).astype(jnp.float32),
        lax.psum_scatter(
            grad_term.astype(jnp.bfloat16), "section", scatter_dimension=1, tiled=True
        ).astype(jnp.float32),
    )
    sigmoid_val = jax.nn.sigmoid(gate_pre)
    activated = gate_pre * sigmoid_val
    hidden = (activated * up_pre).astype(jnp.bfloat16)
    gate_grad = (
        hidden_grad * up_pre * sigmoid_val * (1.0 + gate_pre * (1.0 - sigmoid_val))
    ).astype(jnp.bfloat16)
    up_grad = (hidden_grad * activated).astype(jnp.bfloat16)
    full_hidden, full_gate_grad, full_up_grad = (
        lax.all_gather(hidden, "section", axis=1, tiled=True),
        lax.all_gather(gate_grad, "section", axis=1, tiled=True),
        lax.all_gather(up_grad, "section", axis=1, tiled=True),
    )
    out_rows = jnp.dot(full_hidden, down_w, preferred_element_type=jnp.float32).astype(jnp.bfloat16)
    down_grad = jnp.einsum(
        "rh,rc->hc", full_hidden, routed_grads, preferred_element_type=jnp.float32
    ).astype(jnp.bfloat16)
    slot_grad = jnp.einsum("rh,ch->rc", full_gate_grad, gate_w, preferred_element_type=jnp.float32)
    slot_grad = (
        slot_grad + jnp.einsum("rh,ch->rc", full_up_grad, up_w, preferred_element_type=jnp.float32)
    ).astype(jnp.bfloat16)
    back_out, back_grad = (
        lax.all_to_all(out_rows, "expert", split_axis=0, concat_axis=0, tiled=True),
        lax.all_to_all(slot_grad, "expert", split_axis=0, concat_axis=0, tiled=True),
    )
    picked_out = jnp.dot(picker.astype(jnp.bfloat16), back_out, preferred_element_type=jnp.float32)
    picked_out = picked_out.reshape(tok_rows, top_count, col_span)
    mixed = jnp.sum(gates[:, :, None] * picked_out, axis=1).astype(jnp.bfloat16)
    token_grads = jnp.dot(
        chooser.astype(jnp.bfloat16), back_grad, preferred_element_type=jnp.float32
    ).astype(jnp.bfloat16)
    return (mixed, token_grads, down_grad[None])


MESH = pl.DeviceIdType.MESH
GROUPS = 4
ORDER = (0, 2, 1, 3)
DISPATCH = (2, 0, 1, 3)
STEPS = (
    "A0", "B0", "A2", "B2", "C0", "C2", "A3", "D0", "B3", "D2",
    "E2", "E0", "C3", "A1", "D3", "B1", "E3", "A4", "C1", "B4",
    "A5", "D1", "C4", "B5", "E1", "D4", "C5", "E4", "D5", "E5",
)
NT = (((1,), (1,)), ((), ()))
TN = (((0,), (0,)), ((), ()))
F32 = jnp.float32
BF = jnp.bfloat16


def expert_kernel(
    n_exp, cap, ids_r, gate_r, tok, cot, wg_h, wu_h, wd_h,
    back, dg_o,
    wg, wu, wd, send, recv, part, r1, s2, r2, act, hbuf, obuf, dgbuf,
    w_sem, d_ss, d_rs, s1_ss, s1_rs, s2_ss, s2_rs, gy_ss, gy_rs, gm_ss, gm_rs,
    gr_ss, gr_rs, b_ss, b_rs, loc_sem, o_sem,
):
    me_e = lax.axis_index("expert")
    me_s = lax.axis_index("section")
    span = n_exp // GROUPS
    my_g, my_x = me_e // span, me_e % span
    my_y, my_c = me_s // 2, me_s % 2
    oth_y, oth_c = 1 - my_y, 1 - my_c
    mate = my_y * 2 + oth_c
    ypart = oth_y * 2 + my_c
    rows = span * cap
    slots = n_exp * cap
    n_tok, cols = tok.shape
    quarter = part.shape[-1]
    topk = ids_r.shape[0]

    def group_of(c):
        return ((my_g // 2 + c // 2) % 2) * 2 + (my_g % 2 + c % 2) % 2

    def peers(c):
        return [group_of(c) * span + (my_x + i) % span for i in range(span)]

    loads = [
        pltpu.make_async_copy(a, b, w_sem.at[i])
        for i, (a, b) in enumerate(((wg_h, wg), (wu_h, wu), (wd_h, wd)))
    ]
    for load in loads:
        load.start()

    barrier = pltpu.get_barrier_semaphore()
    for i in range(1, n_exp):
        pl.semaphore_signal(
            barrier, inc=1, device_id=(me_s, (me_e + i) % n_exp), device_id_type=MESH
        )
    for s in (mate, ypart):
        pl.semaphore_signal(barrier, inc=1, device_id=(s, me_e), device_id_type=MESH)

    e_r = lax.broadcasted_iota(jnp.int32, (n_exp, n_tok), 0)
    hot_r = [(ids_r[k : k + 1, :] == e_r).astype(F32) for k in range(topk)]
    t0 = lax.broadcasted_iota(jnp.int32, (n_tok, n_tok), 0)
    t1 = lax.broadcasted_iota(jnp.int32, (n_tok, n_tok), 1)
    earlier_r = jnp.dot(
        sum(hot_r).astype(BF), (t0 < t1).astype(BF), preferred_element_type=F32
    )
    def dispatch(peer):
        return pltpu.make_async_remote_copy(
            src_ref=send.at[peer], dst_ref=recv.at[me_e], send_sem=d_ss.at[peer],
            recv_sem=d_rs.at[me_e], device_id=(me_s, peer), device_id_type=MESH,
        )

    def arrived(peer):
        return pltpu.make_async_remote_copy(
            src_ref=send.at[peer], dst_ref=recv.at[peer], send_sem=d_ss.at[peer],
            recv_sem=d_rs.at[peer], device_id=(me_s, peer), device_id_type=MESH,
        )

    def give(peer):
        return pltpu.make_async_remote_copy(
            src_ref=obuf.at[peer], dst_ref=back.at[me_e], send_sem=b_ss.at[peer],
            recv_sem=b_rs.at[me_e], device_id=(me_s, peer), device_id_type=MESH,
        )

    def given(peer):
        return pltpu.make_async_remote_copy(
            src_ref=obuf.at[peer], dst_ref=back.at[peer], send_sem=b_ss.at[peer],
            recv_sem=b_rs.at[peer], device_id=(me_s, peer), device_id_type=MESH,
        )

    def to_section(src, dst, ss, rs, s):
        return pltpu.make_async_remote_copy(
            src_ref=src, dst_ref=dst, send_sem=ss, recv_sem=rs,
            device_id=(s, me_e), device_id_type=MESH,
        )

    slot_r = []
    for k in range(topk):
        base = earlier_r + sum(hot_r[:k], jnp.zeros_like(earlier_r))
        slot_k = jnp.sum(hot_r[k] * (base + e_r.astype(F32) * cap), axis=0, keepdims=True)
        slot_r.append(slot_k.astype(jnp.int32))
    s_iota = lax.broadcasted_iota(jnp.int32, (rows, n_tok), 0)
    own = pltpu.make_async_copy(send.at[me_e], recv.at[me_e], loc_sem.at[0])
    for c in DISPATCH:
        first = group_of(c) * span
        chooser = jnp.zeros((rows, n_tok), F32)
        gcol = jnp.zeros((rows, 1), F32)
        for k in range(topk):
            hit = (slot_r[k] - first * cap == s_iota).astype(F32)
            chooser = chooser + hit
            gcol = gcol + jnp.sum(hit * gate_r[k : k + 1, :], axis=1, keepdims=True)
        chooser = chooser.astype(BF)
        picked = jnp.dot(chooser, tok[...], preferred_element_type=F32).astype(BF)
        send[pl.ds(first, span), 0] = picked.reshape(span, cap, cols)
        picked = (jnp.dot(chooser, cot[...], preferred_element_type=F32) * gcol).astype(BF)
        send[pl.ds(first, span), 1] = picked.reshape(span, cap, cols)
        if c == DISPATCH[0]:
            pl.semaphore_wait(barrier, n_exp + 1)
        for i, peer in enumerate(peers(c)):
            if c or i:
                dispatch(peer).start()
            else:
                own.start()
    for load in loads:
        load.wait()

    def blocks(ch):
        c, i, n = ch
        return pl.ds(c * span + i, n)

    def first_of(ch):
        c, i, n = ch
        return group_of(c) * span + (0 if n == span else (my_x + i) % span)

    def members(ch):
        c, i, n = ch
        return [(c == 0 and j == 0, peers(c)[j]) for j in range(i, i + n)]

    def sem_of(ch):
        return ch[0] * span + ch[1]

    def rs1(ch):
        b, k = blocks(ch), sem_of(ch)
        return to_section(part.at[b, oth_c], r1.at[b], s1_ss.at[k], s1_rs.at[k], mate)

    def rs2(ch):
        b, k = blocks(ch), sem_of(ch)
        return to_section(s2.at[b], r2.at[b], s2_ss.at[k], s2_rs.at[k], ypart)

    def ag_y(ch, y=None):
        k = sem_of(ch)
        mine = act.at[blocks(ch), my_c, my_y if y is None else y]
        return to_section(mine, mine, gy_ss.at[k], gy_rs.at[k], ypart)

    def ag_m(ch, core=None):
        k = sem_of(ch)
        mine = act.at[blocks(ch), my_c if core is None else core, my_y]
        return to_section(mine, mine, gm_ss.at[k], gm_rs.at[k], mate)

    def ag_r(ch, core=None):
        k = sem_of(ch)
        mine = act.at[blocks(ch), my_c if core is None else core, oth_y]
        return to_section(mine, mine, gr_ss.at[k], gr_rs.at[k], mate)

    def stage_a(ch):
        n = ch[2]
        for here, peer in members(ch):
            if here:
                own.wait()
            else:
                arrived(peer).wait_recv()
        first = first_of(ch)
        x = recv[pl.ds(first, n), 0].reshape(n * cap, cols)
        g = recv[pl.ds(first, n), 1].reshape(n * cap, cols)
        for q in range(4):
            at = slice(q * quarter, (q + 1) * quarter)
            terms = (
                jnp.dot(x, wg[:, at], preferred_element_type=F32),
                jnp.dot(x, wu[:, at], preferred_element_type=F32),
                lax.dot_general(g, wd[at, :], NT, preferred_element_type=F32),
            )
            for j in range(3):
                part[blocks(ch), q // 2, q % 2, j] = (
                    terms[j].astype(BF).reshape(n, cap, quarter)
                )
        rs1(ch).start()

    def stage_b(ch):
        b = blocks(ch)
        rs1(ch).wait_recv()
        s2[b] = (part[b, my_c, oth_y].astype(F32) + r1[b, oth_y].astype(F32)).astype(BF)
        rs2(ch).start()

    def stage_c(ch):
        b = blocks(ch)
        rs2(ch).wait_recv()

        def total(j):
            return (
                part[b, my_c, my_y, j].astype(F32) + r1[b, my_y, j].astype(F32)
                + r2[b, j].astype(F32)
            )

        pre, up, hg = total(0), total(1), total(2)
        sig = jax.nn.sigmoid(pre)
        silu = pre * sig
        act[b, my_c, my_y, 0] = (silu * up).astype(BF)
        act[b, my_c, my_y, 1] = (hg * up * sig * (1.0 + pre * (1.0 - sig))).astype(BF)
        act[b, my_c, my_y, 2] = (hg * silu).astype(BF)
        ag_y(ch).start()
        ag_m(ch).start()

    def stage_d(ch):
        ag_y(ch, oth_y).wait_recv()
        ag_r(ch).start()

    def stage_e(ch):
        n = ch[2]
        ag_m(ch, oth_c).wait_recv()
        ag_r(ch, oth_c).wait_recv()
        h, gg, ug = [
            jnp.concatenate(
                [
                    act[blocks(ch), q // 2, q % 2, j].reshape(n * cap, quarter)
                    for q in range(4)
                ],
                axis=1,
            )
            for j in range(3)
        ]
        first = first_of(ch)
        hbuf[pl.ds(first, n)] = h.reshape(n, cap, 4 * quarter)
        out = jnp.dot(h, wd[...], preferred_element_type=F32).astype(BF)
        obuf[pl.ds(first, n), 0] = out.reshape(n, cap, cols)
        sg = lax.dot_general(gg, wg[...], NT, preferred_element_type=F32)
        sg = (sg + lax.dot_general(ug, wu[...], NT, preferred_element_type=F32)).astype(BF)
        obuf[pl.ds(first, n), 1] = sg.reshape(n, cap, cols)
        for here, peer in members(ch):
            if here:
                pltpu.make_async_copy(obuf.at[me_e], back.at[me_e], loc_sem.at[1]).start()
            else:
                give(peer).start()

    stages = {"A": stage_a, "B": stage_b, "C": stage_c, "D": stage_d, "E": stage_e}
    near = {"0": (0, 0, span), "1": (1, 0, span)}
    half = span // 2
    far = {
        "2": (2, 0, half), "3": (2, half, half), "4": (3, 0, half), "5": (3, half, half)
    }
    chunks = {**near, **far}
    for step in STEPS:
        stages[step[0]](chunks[step[1]])

    store = pltpu.make_async_copy(dgbuf, dg_o, o_sem)
    all_g = recv[:, 1].reshape(slots, cols)
    for q in range(4):
        at = slice(q * quarter, (q + 1) * quarter)
        hq = hbuf[:, :, at].reshape(slots, quarter)
        dgbuf[at, :] = lax.dot_general(hq, all_g, TN, preferred_element_type=F32).astype(BF)
    store.start()

    for c in ORDER:
        for i, peer in enumerate(peers(c)):
            if c or i:
                given(peer).wait_recv()
            else:
                pltpu.make_async_copy(obuf.at[me_e], back.at[me_e], loc_sem.at[1]).wait()
    for c in ORDER:
        for i, peer in enumerate(peers(c)):
            if c or i:
                dispatch(peer).wait_send()
                give(peer).wait_send()
    for ch in chunks.values():
        for copy in (rs1(ch), rs2(ch), ag_y(ch), ag_m(ch), ag_r(ch)):
            copy.wait_send()
    store.wait()


def combine_kernel(n_exp, cap, ids_r, gate_r, back_h, dg_h, mixed_o, tgrad_o, dg_o, back, dg, sem):
    topk, n_tok = ids_r.shape
    hid, cols = dg.shape
    slots = n_exp * cap
    part = hid // GROUPS
    half = n_exp // 2
    gets = [
        pltpu.make_async_copy(
            back_h.at[pl.ds(i * half, half)], back.at[pl.ds(i * half, half)], sem.at[i]
        )
        for i in range(2)
    ]
    ins = [
        pltpu.make_async_copy(
            dg_h.at[pl.ds(i * part, part)], dg.at[pl.ds(i * part, part)], sem.at[2 + i]
        )
        for i in range(GROUPS)
    ]
    outs = [
        pltpu.make_async_copy(
            dg.at[pl.ds(i * part, part)], dg_o.at[pl.ds(i * part, part)], sem.at[2 + GROUPS + i]
        )
        for i in range(GROUPS)
    ]
    for get in gets + ins:
        get.start()
    t0 = lax.broadcasted_iota(jnp.int32, (n_tok, n_tok), 0)
    t1 = lax.broadcasted_iota(jnp.int32, (n_tok, n_tok), 1)
    eye = (t0 == t1).astype(F32)
    e_r = lax.broadcasted_iota(jnp.int32, (n_exp, n_tok), 0)
    hot = [(ids_r[k : k + 1, :] == e_r).astype(F32) for k in range(topk)]
    earlier = jnp.dot(sum(hot).astype(BF), (t0 < t1).astype(BF), preferred_element_type=F32)
    l_iota = lax.broadcasted_iota(jnp.int32, (n_tok, slots), 1)
    picks, weights = [], []
    for k in range(topk):
        base = earlier + sum(hot[:k], jnp.zeros_like(earlier))
        slot_k = jnp.sum(hot[k] * (base + e_r.astype(F32) * cap), axis=0, keepdims=True)
        column = jnp.sum(eye * slot_k, axis=1, keepdims=True).astype(jnp.int32)
        picks.append((column == l_iota).astype(F32))
        weights.append(jnp.sum(eye * gate_r[k : k + 1, :], axis=1, keepdims=True))
    for get in gets:
        get.wait()
    for i in range(GROUPS):
        ins[i].wait()
        outs[i].start()
    rows_out = back[:, 0].reshape(slots, cols)
    mixed = sum(
        weights[k] * jnp.dot(picks[k].astype(BF), rows_out, preferred_element_type=F32)
        for k in range(topk)
    )
    mixed_o[...] = mixed.astype(BF)
    tgrad_o[...] = jnp.dot(
        sum(picks).astype(BF), back[:, 1].reshape(slots, cols), preferred_element_type=F32
    ).astype(BF)
    for put in outs:
        put.wait()


def fused(tokens, expert_ids, gates, cotangent, w_gate, w_up, w_down):
    n_tok, topk = expert_ids.shape
    cols = tokens.shape[1]
    hid = w_gate.shape[2]
    n_exp, n_sec = lax.axis_size("expert"), lax.axis_size("section")
    cap = capacity_of(n_tok, topk, n_exp)
    quarter = hid // n_sec
    vm = pl.BlockSpec(memory_space=pltpu.VMEM)
    hbm = pl.BlockSpec(memory_space=pl.ANY)
    dma = pltpu.SemaphoreType.DMA
    per = (n_exp, 2, 2, 3, cap, quarter)
    ids_r, gate_r = expert_ids.T, gates.T
    back, dg = pl.pallas_call(
        functools.partial(expert_kernel, n_exp, cap),
        out_shape=(
            jax.ShapeDtypeStruct((n_exp, 2, cap, cols), BF),
            jax.ShapeDtypeStruct((hid, cols), BF),
        ),
        in_specs=[vm] * 4 + [hbm] * 3,
        out_specs=(hbm, hbm),
        scratch_shapes=[
            pltpu.VMEM((cols, hid), BF),
            pltpu.VMEM((cols, hid), BF),
            pltpu.VMEM((hid, cols), BF),
            pltpu.VMEM((n_exp, 2, cap, cols), BF),
            pltpu.VMEM((n_exp, 2, cap, cols), BF),
            pltpu.VMEM(per, BF),
            pltpu.VMEM((n_exp, 2, 3, cap, quarter), BF),
            pltpu.VMEM((n_exp, 3, cap, quarter), BF),
            pltpu.VMEM((n_exp, 3, cap, quarter), BF),
            pltpu.VMEM(per, BF),
            pltpu.VMEM((n_exp, cap, hid), BF),
            pltpu.VMEM((n_exp, 2, cap, cols), BF),
            pltpu.VMEM((hid, cols), BF),
            dma((3,)),
            dma((n_exp,)), dma((n_exp,)),
        ]
        + [dma((n_exp,)) for _ in range(10)]
        + [dma((n_exp,)), dma((n_exp,)), dma((2,)), dma],
        compiler_params=pltpu.CompilerParams(
            collective_id=0, has_side_effects=True, vmem_limit_bytes=60 * 1024 * 1024
        ),
    )(ids_r, gate_r, tokens, cotangent, w_gate[0], w_up[0], w_down[0])
    mixed, tgrad, dg = pl.pallas_call(
        functools.partial(combine_kernel, n_exp, cap),
        out_shape=(
            jax.ShapeDtypeStruct((n_tok, cols), BF),
            jax.ShapeDtypeStruct((n_tok, cols), BF),
            jax.ShapeDtypeStruct((hid, cols), BF),
        ),
        in_specs=[vm] * 2 + [hbm] * 2,
        out_specs=(vm, vm, hbm),
        scratch_shapes=[
            pltpu.VMEM((n_exp, 2, cap, cols), BF),
            pltpu.VMEM((hid, cols), BF),
            dma((2 + 2 * GROUPS,)),
        ],
        compiler_params=pltpu.CompilerParams(vmem_limit_bytes=60 * 1024 * 1024),
    )(ids_r, gate_r, back, dg)
    return mixed, tgrad, dg[None]


def capacity_of(tok_rows, top_count, expert_count):
    return min(tok_rows, max(2, 3 * tok_rows * top_count // (2 * expert_count)))


def layer(tokens, expert_ids, *rest):
    n_exp, n_sec = lax.axis_size("expert"), lax.axis_size("section")
    n_tok, topk = expert_ids.shape
    cap = capacity_of(n_tok, topk, n_exp)
    hid = rest[2].shape[2]
    tiles = (
        n_exp == 2 * GROUPS and n_sec == 4 and cap % 16 == 0 and n_tok % 128 == 0
        and tokens.shape[1] % 128 == 0 and hid % (n_sec * 128) == 0
    )
    return (fused if tiles else local)(tokens, expert_ids, *rest)


def solution(mesh):
    placed = (
        P("expert", "section"),
        P("expert", None),
        P("expert", None),
        P("expert", "section"),
        P("expert", "section", None),
        P("expert", "section", None),
        P("expert", None, "section"),
    )
    return jax.shard_map(
        layer,
        mesh=mesh,
        in_specs=placed,
        out_specs=(P("expert", "section"), P("expert", "section"), P("expert", None, "section")),
        check_vma=False,
    )
```
